512 devices in a mesh: panel: 8 (over x, core), sc: 64 (over z, y).
Axes of the slice: x: 4, y: 8, z: 8, core: 2. Of those that a mesh axis runs over, the one named last changes fastest.
Arguments:
- channel: bfloat16 [2, 2048, 1024, 128], P(None, 'sc', 'panel'), may hold values from -0.1875 to 0.1875
- received: bfloat16 [2, 2048, 1024], P(None, 'sc', 'panel'), may hold values from -6 to 6
- noise: float32 [2048], P('sc'), may hold values from 0.05 to 0.5
- steps: float32 [3, 2, 128, 128], replicated, may hold values from -0.5 to 0.5
- cotangent: float32 [2, 2048, 128], P(None, 'sc', 'panel'), may hold values from -6 to 6
- counts: int32 [64], P('sc'), may hold values from 1 to 32, 1280 in all
Outputs:
- grad_channel: bfloat16 [2, 2048, 1024, 128], P(None, 'sc', 'panel')
- grad_received: bfloat16 [2, 2048, 1024], P(None, 'sc', 'panel')
- grad_steps: float32 [3, 2, 128, 128], replicated
The draws below stay inside these ranges and needn't reach their ends.
Inputs may be any that keep to these rules, and one draw needn't show every extreme that they name: `counts`: each block has between 1 and 32 rostered subcarriers, and some block has all 32.
All inputs are finite; a program needn't handle non-finite values.
Results may differ from the reference program's by a relative error of at most 0.014.
Values may be sent and summed in bfloat16 or wider, within the bound.
No kernel may reach another device: no remote copies, remote signals or barrier semaphores. Data moves between devices by JAX's collectives and lax.ppermute only.
A program may use at most 64 MiB of HBM per device.

```python
import math
import jax
import jax.numpy as jnp
import numpy as np
from jax import lax

A = 1024
U = 128
ITERS = 3
SC_DEV = 32
S = 2048
N_SC = 64


def block_scale(stream_key, shape, split, low, largest):
    def one(axis_at, shards_of):
        draws = jax.random.uniform(jax.random.fold_in(jax.random.fold_in(stream_key, 6), axis_at), (shards_of,), jnp.float32, low / len(split), largest / len(split))
        return jnp.repeat(jnp.exp(draws), shape[axis_at] // shards_of).reshape((-1,) + (1,) * (len(shape) - axis_at - 1))

    loudness = one(*split[0])
    for cut in split[1:]:
        loudness = loudness * one(*cut)
    return loudness


def length_profile(count, total, reach, lean):
    portions = [(1 << 20) // math.isqrt(standing ** lean) + 1 for standing in range(2, count + 1)]
    rest, holding = total - reach - (count - 1), [1] * (count - 1)
    while rest > 0:
        free = [i for i in range(count - 1) if holding[i] < reach]
        mass, remaining = sum([portions[i] for i in free]), rest
        for i in free:
            more = min(reach - holding[i], max(1, remaining * portions[i] // mass), rest)
            holding[i] = holding[i] + more
            rest = rest - more
    return np.array([reach] + holding)


def uneven_parts(stream_key, number_of, total, limit, skew):
    if number_of == 2:
        one = jax.random.randint(stream_key, (), max(1, total - limit), min(limit, total - 1) + 1)
        return jnp.stack([one, total - one])
    lengths = jnp.asarray(length_profile(number_of, total, limit, skew), jnp.int32)
    couples = (number_of - 1) // 2
    source_of, receiver = lengths[1:1 + 2 * couples:2], lengths[2:2 + 2 * couples:2]
    margin = jnp.minimum(source_of - 1, limit - receiver)
    moved = jax.random.randint(jax.random.fold_in(stream_key, 1), (couples,), 0, 1 << 20) % (margin + 1)
    lengths = lengths.at[1:1 + 2 * couples:2].set(source_of - moved).at[2:2 + 2 * couples:2].set(receiver + moved)
    return lengths[jax.random.permutation(jax.random.fold_in(stream_key, 2), number_of)]


def normal_values(key, extent, spread, most, cuts=(), held_as=jnp.bfloat16):
    entries = jax.random.normal(key, extent, jnp.float32) * spread
    if len(cuts) > 0:
        entries = block_scale(key, extent, cuts, -0.22, 0.18) * entries
    return jnp.clip(entries, min=-most, max=most).astype(held_as)


def setup_inputs(seed: int = 0) -> dict:
    arg_keys = jax.random.split(jax.random.key(seed), 7)
    channel = normal_values(arg_keys[0], (2, S, A, U), A ** -0.5, 0.1875, ((1, 64), (2, 8)))
    received = normal_values(arg_keys[1], (2, S, A), 1.0, 6.0, ((1, 64), (2, 8)))
    noise = jnp.clip(jnp.exp(math.log(0.5) - 2.3025851 * jax.random.uniform(arg_keys[2], (S,), jnp.float32) ** block_scale(arg_keys[2], (S,), ((0, 64),), -0.2, 0.2)), 0.05, 0.5)
    steps = normal_values(arg_keys[3], (ITERS, 2, U, U), U ** -0.5, 0.5, (), jnp.float32)
    cotangent = normal_values(arg_keys[4], (2, S, U), 1.0, 6.0, ((1, 64), (2, 8)), jnp.float32)
    counts = uneven_parts(arg_keys[5], N_SC, SC_DEV * N_SC * 5 // 8, SC_DEV, 2).astype(jnp.int32)
    return dict(channel=channel, received=received, noise=noise, steps=steps, cotangent=cotangent, counts=counts)


EPS = 1e-06

def batched(matrix, vector):
    return jnp.einsum('suv,sv->su', matrix, vector, precision=lax.Precision.HIGHEST)

def shared(matrix, vector):
    return jnp.einsum('uv,sv->su', matrix, vector, precision=lax.Precision.HIGHEST)

def detector(gram_re, gram_im, match_re, match_im, steps, noise):
    sol_re = jnp.zeros_like(match_re)
    sol_im = jnp.zeros_like(match_im)
    resid_re, resid_im = (match_re, match_im)
    energy = lax.optimization_barrier(jnp.sum(resid_re * resid_re + resid_im * resid_im, axis=1)) + EPS
    earlier = energy
    prev_re, prev_im = (sol_re, sol_im)
    for index in range(steps.shape[0]):
        w_re, w_im = (steps[index, 0], steps[index, 1])
        dir_re = resid_re + shared(w_re, resid_re) - shared(w_im, resid_im)
        dir_im = resid_im + shared(w_re, resid_im) + shared(w_im, resid_re)
        if index > 0:
            ratio = (energy / earlier)[:, None]
            dir_re = dir_re + ratio * prev_re
            dir_im = dir_im + ratio * prev_im
        img_re = batched(gram_re, dir_re) - batched(gram_im, dir_im) + noise[:, None] * dir_re
        img_im = batched(gram_re, dir_im) + batched(gram_im, dir_re) + noise[:, None] * dir_im
        along = lax.optimization_barrier(jnp.sum(dir_re * resid_re + dir_im * resid_im, axis=1))
        curvature = lax.optimization_barrier(jnp.sum(dir_re * img_re + dir_im * img_im, axis=1)) + EPS
        alpha = (along / curvature)[:, None]
        sol_re = sol_re + alpha * dir_re
        sol_im = sol_im + alpha * dir_im
        resid_re = resid_re - alpha * img_re
        resid_im = resid_im - alpha * img_im
        earlier = energy
        energy = lax.optimization_barrier(jnp.sum(resid_re * resid_re + resid_im * resid_im, axis=1)) + EPS
        prev_re, prev_im = (dir_re, dir_im)
    return (sol_re, sol_im)

def inner(form, left, right):
    return jnp.einsum(form, left.astype(jnp.float32), right.astype(jnp.float32), precision=lax.Precision.HIGHEST)

def block_grad(inputs):
    chan, recv, noise_blk, cot_blk, live, steps = inputs
    h_re, h_im = (chan[0], chan[1])
    y_re, y_im = (recv[0], recv[1])
    gram_re = inner('sau,sav->suv', h_re, h_re) + inner('sau,sav->suv', h_im, h_im)
    gram_im = inner('sau,sav->suv', h_re, h_im) - inner('sau,sav->suv', h_im, h_re)
    match_re = inner('sau,sa->su', h_re, y_re) + inner('sau,sa->su', h_im, y_im)
    match_im = inner('sau,sa->su', h_re, y_im) - inner('sau,sa->su', h_im, y_re)

    def forward(g_re, g_im, m_re, m_im, w_all):
        return detector(g_re, g_im, m_re, m_im, w_all, noise_blk)
    outputs, pullback = jax.vjp(forward, gram_re, gram_im, match_re, match_im, steps)
    grads = pullback((cot_blk[0] * live[:, None], cot_blk[1] * live[:, None]))
    sym = (grads[0] + jnp.swapaxes(grads[0], 1, 2)).astype(jnp.bfloat16)
    anti = (grads[1] - jnp.swapaxes(grads[1], 1, 2)).astype(jnp.bfloat16)
    back_re = grads[2].astype(jnp.bfloat16).astype(jnp.float32)
    back_im = grads[3].astype(jnp.bfloat16).astype(jnp.float32)
    yr32 = y_re.astype(jnp.float32)
    yi32 = y_im.astype(jnp.float32)
    grad_hre = inner('sav,svu->sau', h_re, sym) - inner('sav,svu->sau', h_im, anti)
    grad_hre = grad_hre + yr32[:, :, None] * back_re[:, None, :] + yi32[:, :, None] * back_im[:, None, :]
    grad_him = inner('sav,svu->sau', h_im, sym) + inner('sav,svu->sau', h_re, anti)
    grad_him = grad_him + yi32[:, :, None] * back_re[:, None, :] - yr32[:, :, None] * back_im[:, None, :]
    grad_yre = inner('sau,su->sa', h_re, back_re) - inner('sau,su->sa', h_im, back_im)
    grad_yim = inner('sau,su->sa', h_im, back_re) + inner('sau,su->sa', h_re, back_im)
    grad_chan = jnp.stack([grad_hre, grad_him]).astype(jnp.bfloat16)
    grad_recv = jnp.stack([grad_yre, grad_yim]).astype(jnp.bfloat16)
    return (grad_chan, grad_recv, grads[4])

def reference(channel, received, noise, steps, cotangent, counts):
    blocks = N_SC
    chan_blocks = channel.reshape(2, blocks, SC_DEV, A, U).transpose(1, 0, 2, 3, 4)
    recv_blocks = received.reshape(2, blocks, SC_DEV, A).transpose(1, 0, 2, 3)
    noise_blocks = noise.reshape(blocks, SC_DEV)
    cot_blocks = cotangent.reshape(2, blocks, SC_DEV, U).transpose(1, 0, 2, 3)
    position = jnp.arange(SC_DEV, dtype=jnp.int32)
    live = (position[None, :] < counts[:, None]).astype(jnp.float32)

    def one_block(inputs):
        chan, recv, noise_blk, cot_blk, live_blk = inputs
        return block_grad((chan, recv, noise_blk, cot_blk, live_blk, steps))
    grad_chan, grad_recv, grad_w = lax.map(one_block, (chan_blocks, recv_blocks, noise_blocks, cot_blocks, live))
    grad_channel = grad_chan.transpose(1, 0, 2, 3, 4).reshape(2, S, A, U)
    grad_received = grad_recv.transpose(1, 0, 2, 3).reshape(2, S, A)
    return (grad_channel, grad_received, lax.optimization_barrier(jnp.sum(grad_w, axis=0)))
```

```python
import functools

import jax
import jax.numpy as jnp
from jax import lax
from jax.experimental import pallas as pl
from jax.experimental.pallas import tpu as pltpu
from jax.sharding import PartitionSpec as P

EPS = 1e-06
F32 = jnp.float32
BF16 = jnp.bfloat16
NP = 8
SUB = 4
U = 128
A = 128
ROWS = 144
NN = (((1,), (0,)), ((), ()))
NT = (((1,), (1,)), ((), ()))
TN = (((0,), (0,)), ((), ()))


def dot(left, right, dims=NN):
    return lax.dot_general(left, right, dims, preferred_element_type=F32)


def split(value):
    high = value.astype(BF16)
    return high, (value - high.astype(F32)).astype(BF16)


def iota(shape, axis):
    return lax.broadcasted_iota(jnp.int32, shape, axis)


def rows_of(pieces, count):
    width = pieces[0][0].shape[1]
    at = iota((count, width), 0)
    out = jnp.zeros((count, width), F32)
    for k, (array, row) in enumerate(pieces):
        out = jnp.where(at == k, jnp.broadcast_to(array[row : row + 1], (count, width)), out)
    return out


def gram_kernel(chan_ref, recv_ref, cot_ref, out_ref, cot_rows):
    panel = lax.axis_index("panel")
    step = pl.program_id(0)

    @pl.when(step == 0)
    def _():
        place = (iota((16, U), 1) == panel * 16 + iota((16, U), 0)).astype(F32).astype(BF16)
        for part in range(2):
            high, low = split(cot_ref[part])
            cot_rows[2 * part] = dot(high, place, TN)
            cot_rows[2 * part + 1] = dot(low, place, TN)

    y_rows = jnp.concatenate([recv_ref[0], recv_ref[1]], axis=1)
    y_rows = jnp.concatenate([y_rows, jnp.zeros_like(y_rows)], axis=0)
    here = pl.ds(pl.multiple_of(step * 8, 8), 8)
    cots = [cot_rows[k, here, :] for k in range(4)]
    upper = iota((U, U), 0) <= iota((U, U), 1)
    for j in range(8):
        h_re, h_im = chan_ref[0, j], chan_ref[1, j]
        stack = jnp.concatenate([h_re, h_im], axis=0)
        other = jnp.concatenate([h_im, -h_re], axis=0)
        both = jnp.concatenate([stack, other], axis=1)
        left = jnp.concatenate([stack.T, y_rows], axis=0)
        prod = dot(left, both)
        packed = jnp.where(upper, prod[:U, :U], prod[:U, U:])
        match = prod[U + j : U + j + 1]
        m_re, m_im = match[:, :U], -match[:, U:]
        m_re_high, m_im_high = m_re.astype(BF16).astype(F32), m_im.astype(BF16).astype(F32)
        extra = rows_of(
            [(m_re_high, 0), (m_re - m_re_high, 0), (m_im_high, 0), (m_im - m_im_high, 0)]
            + [(c, j) for c in cots],
            16,
        )
        out_ref[j // SUB, j % SUB, 0:U, :] = packed.astype(BF16)
        out_ref[j // SUB, j % SUB, U:ROWS, :] = extra.astype(BF16)


def gram_call(channel, received, cot):
    return pl.pallas_call(
        gram_kernel,
        grid=(4,),
        out_shape=jax.ShapeDtypeStruct((NP, SUB, ROWS, U), BF16),
        in_specs=[
            pl.BlockSpec((2, 8, A, U), lambda i: (0, i, 0, 0)),
            pl.BlockSpec((2, 8, A), lambda i: (0, i, 0)),
            pl.BlockSpec((2, 16, 32), lambda i: (0, 0, 0)),
        ],
        out_specs=pl.BlockSpec((2, SUB, ROWS, U), lambda i: (i, 0, 0, 0)),
        scratch_shapes=[pltpu.VMEM((4, 32, U), F32)],
        name="gram",
    )(channel, received, cot)


def detect_kernel(noise_ref, count_ref, rx_ref, steps_ref, out_ref, gram_w, step_w):
    panel = lax.axis_index("panel")
    for k in range(3):
        w_re, w_im = steps_ref[k, 0], steps_ref[k, 1]
        re_hi, re_lo = split(w_re)
        im_hi, im_lo = split(w_im)
        for n, (re, im) in enumerate(((re_hi, im_hi), (re_lo, im_lo))):
            step_w[k, n, 0:U, 0:U] = re
            step_w[k, n, 0:U, U:] = -im
            step_w[k, n, U:, 0:U] = im
            step_w[k, n, U:, U:] = re
    row, col = iota((U, U), 0), iota((U, U), 1)
    at = iota((8, 2 * U), 0)
    at1 = iota((8, 1), 0)
    match = jnp.zeros((8, 2 * U), F32)
    cot = jnp.zeros((8, 2 * U), F32)
    for s in range(SUB):
        total = rx_ref[0, s].astype(F32)
        for p in range(1, NP):
            total = total + rx_ref[p, s].astype(F32)
        tri = total[0:U]
        flip = tri.T
        g_re = jnp.where(row <= col, tri, flip)
        g_im = jnp.where(row > col, tri, jnp.where(row < col, -flip, 0.0))
        re_hi, re_lo = split(g_re)
        im_hi, im_lo = split(g_im)
        for n, (re, im) in enumerate(((re_hi, im_hi), (re_lo, im_lo))):
            gram_w[s, n, 0:U, 0:U] = re
            gram_w[s, n, 0:U, U:] = -im
            gram_w[s, n, U:, 0:U] = im
            gram_w[s, n, U:, U:] = re
        ext = total[U:ROWS]
        m_row = jnp.concatenate([ext[0:1] + ext[1:2], ext[2:3] + ext[3:4]], axis=1)
        c_row = jnp.concatenate([ext[4:5] + ext[5:6], ext[6:7] + ext[7:8]], axis=1)
        alive = (panel * SUB + s < count_ref[0]).astype(F32)
        match = jnp.where(at == s, jnp.broadcast_to(m_row, (8, 2 * U)), match)
        cot = jnp.where(at == s, jnp.broadcast_to(c_row * alive, (8, 2 * U)), cot)
    sigma = jnp.zeros((8, 1), F32)
    for s in range(SUB):
        sigma = jnp.where(at1 == s, noise_ref[panel * SUB + s], sigma)

    def parts(v):
        high, low = split(v)
        return jnp.concatenate([high, low], axis=0)

    def times_gram(v):
        both = parts(v)
        out = sigma * v
        for s in range(SUB):
            one = dot(both, gram_w[s, 0])
            two = dot(both, gram_w[s, 1])
            out = out + jnp.where(at == s, one[0:8] + one[8:16] + two[0:8], 0.0)
        return out

    def times_step(k, v, dims):
        both = parts(v)
        one = dot(both, step_w[k, 0], dims)
        two = dot(both, step_w[k, 1], dims)
        return one[0:8] + one[8:16] + two[0:8]

    def total_of(a, b):
        return jnp.sum(a * b, axis=1, keepdims=True)

    r = match
    energy = total_of(r, r) + EPS
    rs, ds, qs, es, al, cs, bs = [], [], [], [energy], [], [], []
    for k in range(3):
        d = r + times_step(k, r, NT)
        ratio = None
        if k > 0:
            ratio = es[k] / es[k - 1]
            d = d + ratio * ds[-1]
        q = times_gram(d)
        along = total_of(d, r)
        curve = total_of(d, q) + EPS
        alpha = along / curve
        rs.append(r)
        ds.append(d)
        qs.append(q)
        al.append(alpha)
        cs.append(curve)
        bs.append(ratio)
        if k < 2:
            r = r - alpha * q
            es.append(total_of(r, r) + EPS)

    qb, db = [None] * 3, [None] * 3
    rb = None
    d_next = None
    e_bar = [jnp.zeros((8, 1), F32) for _ in range(3)]
    for k in (2, 1, 0):
        a_bar = total_of(cot, ds[k])
        if rb is not None:
            a_bar = a_bar - total_of(rb, qs[k])
        along_bar = a_bar / cs[k]
        curve_bar = -along_bar * al[k]
        d_bar = al[k] * cot + along_bar * rs[k] + curve_bar * qs[k]
        if d_next is not None:
            d_bar = d_bar + d_next
        if rb is None:
            qb[k] = curve_bar * ds[k]
            d_bar = d_bar + curve_bar * qs[k]
            rb = along_bar * ds[k]
        else:
            qb[k] = curve_bar * ds[k] - al[k] * rb
            d_bar = d_bar + times_gram(qb[k])
            rb = rb + along_bar * ds[k]
        db[k] = d_bar
        rb = rb + d_bar + times_step(k, d_bar, NN)
        if k > 0:
            b_bar = total_of(d_bar, ds[k - 1]) / es[k - 1]
            e_bar[k] = e_bar[k] + b_bar
            e_bar[k - 1] = e_bar[k - 1] - b_bar * bs[k]
            d_next = bs[k] * d_bar
        rb = rb + 2.0 * e_bar[k] * rs[k]

    for s in range(SUB):
        block = rows_of([(v, s) for v in (qb[0], ds[0], qb[1], ds[1], qb[2], ds[2], rb)], 8)
        both = jnp.concatenate([block[:, 0:U], block[:, U:]], axis=0).astype(BF16)
        for p in range(NP):
            out_ref[p, 16 * s : 16 * s + 16, :] = both
    zeros = jnp.zeros((8, 2 * U), F32)
    for k in range(3):
        d_hi, d_lo = split(db[k])
        r_hi, r_lo = split(rs[k])
        left = jnp.concatenate([d_hi, d_lo, d_hi, zeros.astype(BF16)], axis=0)
        right = jnp.concatenate([r_hi, r_hi, r_lo, zeros.astype(BF16)], axis=0)
        outer = dot(left, right, TN)
        g_re = (outer[0:U, 0:U] + outer[U:, U:]).astype(BF16)
        g_im = (outer[U:, 0:U] - outer[0:U, U:]).astype(BF16)
        for p in range(NP):
            base = 64 + k * 32
            out_ref[p, base : base + 16, :] = g_re[16 * p : 16 * p + 16]
            out_ref[p, base + 16 : base + 32, :] = g_im[16 * p : 16 * p + 16]


def detect_call(noise, counts, rx, steps):
    smem = pl.BlockSpec(memory_space=pltpu.SMEM)
    vmem = pl.BlockSpec(memory_space=pltpu.VMEM)
    return pl.pallas_call(
        detect_kernel,
        out_shape=jax.ShapeDtypeStruct((NP, 160, U), BF16),
        in_specs=[smem, smem, vmem, vmem],
        out_specs=vmem,
        scratch_shapes=[
            pltpu.VMEM((SUB, 2, 2 * U, 2 * U), BF16),
            pltpu.VMEM((3, 2, 2 * U, 2 * U), BF16),
        ],
        name="detect",
    )(noise, counts, rx, steps)


def chain_kernel(chan_ref, recv_ref, fac_ref, gchan_ref, grecv_ref):
    at = iota((8, U), 0)
    even = iota((16, U), 0) % 2 == 0
    gy_re = jnp.zeros((8, A), F32)
    gy_im = jnp.zeros((8, A), F32)
    y_re, y_im = recv_ref[0].astype(F32), recv_ref[1].astype(F32)
    for j in range(8):
        s = j % SUB
        fac = fac_ref[j // SUB, 16 * s : 16 * s + 16, :]
        chan = jnp.concatenate([chan_ref[0, j], chan_ref[1, j]], axis=0)
        prod = dot(fac, chan, NT)
        v_re = prod[0:8, 0:A] - prod[8:16, A:]
        v_im = prod[0:8, A:] + prod[8:16, 0:A]
        gy_re = jnp.where(at == j, jnp.broadcast_to(v_re[6:7], (8, A)), gy_re)
        gy_im = jnp.where(at == j, jnp.broadcast_to(v_im[6:7], (8, A)), gy_im)
        v_re = jnp.where(at == 7, jnp.broadcast_to(y_re[j : j + 1], (8, A)), v_re)
        v_im = jnp.where(at == 7, jnp.broadcast_to(y_im[j : j + 1], (8, A)), v_im)
        re_hi, re_lo = split(v_re)
        im_hi, im_lo = split(v_im)
        left = jnp.concatenate([re_hi, im_hi, re_lo, im_lo], axis=0)
        wide = fac.astype(F32)
        down = jnp.concatenate([wide[1:16], wide[0:1]], axis=0)
        up = jnp.concatenate([wide[15:16], wide[0:15]], axis=0)
        mate = jnp.where(even, down, up)
        g_re, g_im = mate[0:8], mate[8:16]
        right = jnp.concatenate(
            [jnp.concatenate([g_re, -g_im], axis=1), jnp.concatenate([g_im, g_re], axis=1)], axis=0
        ).astype(BF16)
        right = jnp.concatenate([right, right], axis=0)
        out = dot(left, right, TN)
        gchan_ref[0, j] = out[:, 0:U].astype(BF16)
        gchan_ref[1, j] = out[:, U:].astype(BF16)
    grecv_ref[0] = gy_re.astype(BF16)
    grecv_ref[1] = gy_im.astype(BF16)


def chain_call(channel, received, factors):
    return pl.pallas_call(
        chain_kernel,
        grid=(4,),
        out_shape=(
            jax.ShapeDtypeStruct((2, 32, A, U), BF16),
            jax.ShapeDtypeStruct((2, 32, A), BF16),
        ),
        in_specs=[
            pl.BlockSpec((2, 8, A, U), lambda i: (0, i, 0, 0)),
            pl.BlockSpec((2, 8, A), lambda i: (0, i, 0)),
            pl.BlockSpec((2, 64, U), lambda i: (i, 0, 0)),
        ],
        out_specs=(
            pl.BlockSpec((2, 8, A, U), lambda i: (0, i, 0, 0)),
            pl.BlockSpec((2, 8, A), lambda i: (0, i, 0)),
        ),
        name="chain",
    )(channel, received, factors)


def exchange(value, axis, groups=None):
    return lax.all_to_all(
        value, axis, split_axis=0, concat_axis=0, tiled=True, axis_index_groups=groups
    )


def on_device(channel, received, noise, steps, cotangent, counts):
    z_groups = [[8 * z + y for z in range(8)] for y in range(8)]
    y_groups = [[8 * z + y for y in range(8)] for z in range(8)]
    sent = gram_call(channel, received, jnp.swapaxes(cotangent, 1, 2))
    rx = exchange(sent, "panel")
    sent = detect_call(noise, counts, rx, steps)
    rx = exchange(sent, "panel")
    grad_channel, grad_received = chain_call(channel, received, rx)
    part = jnp.sum(rx[:, 64:].astype(F32), axis=0).astype(BF16)
    for groups in (y_groups, z_groups):
        every = exchange(jnp.broadcast_to(part, (8, 96, U)), "sc", groups)
        part = jnp.sum(every.astype(F32), axis=0).astype(BF16)
    every = exchange(jnp.broadcast_to(part, (8, 96, U)), "panel")
    grad_steps = every.astype(F32).reshape(8, 6, 16, U).transpose(1, 0, 2, 3)
    return (grad_channel, grad_received, grad_steps.reshape(3, 2, U, U))


def solution(mesh):
    return jax.shard_map(
        on_device,
        mesh=mesh,
        in_specs=(
            P(None, "sc", "panel", None),
            P(None, "sc", "panel"),
            P("sc"),
            P(),
            P(None, "sc", "panel"),
            P("sc"),
        ),
        out_specs=(P(None, "sc", "panel", None), P(None, "sc", "panel"), P()),
        check_vma=False,
    )
```

```python
import functools

import jax
import jax.numpy as jnp
from jax import lax
from jax.experimental import pallas as pl
from jax.experimental.pallas import tpu as pltpu
from jax.sharding import PartitionSpec as P

EPS = 1e-06
F32 = jnp.float32
BF16 = jnp.bfloat16
NP = 8
SUB = 4
U = 128
A = 128
ROWS = 144
NN = (((1,), (0,)), ((), ()))
NT = (((1,), (1,)), ((), ()))
TN = (((0,), (0,)), ((), ()))


def dot(left, right, dims=NN):
    return lax.dot_general(left, right, dims, preferred_element_type=F32)


def split(value):
    high = value.astype(BF16)
    return high, (value - high.astype(F32)).astype(BF16)


def iota(shape, axis):
    return lax.broadcasted_iota(jnp.int32, shape, axis)


def rows_of(pieces, count):
    width = pieces[0][0].shape[1]
    at = iota((count, width), 0)
    out = jnp.zeros((count, width), F32)
    for k, (array, row) in enumerate(pieces):
        out = jnp.where(at == k, jnp.broadcast_to(array[row : row + 1], (count, width)), out)
    return out


def gram_kernel(own, chan_ref, recv_ref, cot_ref, out_ref, cot_rows):
    panel = lax.axis_index("panel")
    step = pl.program_id(0)
    core = lax.rem(panel + (0 if own else 1), 2)

    @pl.when(step == 0)
    def _():
        place = (iota((16, U), 1) == panel * 16 + iota((16, U), 0)).astype(F32).astype(BF16)
        for part in range(2):
            high, low = split(cot_ref[part])
            cot_rows[2 * part] = dot(high, place, TN)
            cot_rows[2 * part + 1] = dot(low, place, TN)

    y_rows = jnp.concatenate([recv_ref[0], recv_ref[1]], axis=1)
    y_rows = jnp.concatenate([y_rows, jnp.zeros_like(y_rows)], axis=0)
    upper = iota((U, U), 0) <= iota((U, U), 1)
    at = iota((8, 2 * U), 0)
    for j in range(SUB):
        row = core * SUB + j
        h_re, h_im = chan_ref[0, row], chan_ref[1, row]
        stack = jnp.concatenate([h_re, h_im], axis=0)
        other = jnp.concatenate([h_im, -h_re], axis=0)
        both = jnp.concatenate([stack, other], axis=1)
        left = jnp.concatenate([stack.T, y_rows], axis=0)
        prod = dot(left, both)
        packed = jnp.where(upper, prod[:U, :U], prod[:U, U:])
        match = jnp.sum(jnp.where(at == row, prod[U : U + 8], 0.0), axis=0, keepdims=True)
        m_re, m_im = match[:, :U], -match[:, U:]
        m_re_high, m_im_high = m_re.astype(BF16).astype(F32), m_im.astype(BF16).astype(F32)
        extra = rows_of(
            [(m_re_high, 0), (m_re - m_re_high, 0), (m_im_high, 0), (m_im - m_im_high, 0)]
            + [(cot_rows[k, pl.ds(step * 8 + row, 1), :], 0) for k in range(4)],
            16,
        )
        out_ref[0, j, 0:U, :] = packed.astype(BF16)
        out_ref[0, j, U:ROWS, :] = extra.astype(BF16)


def gram_call(own, channel, received, cot):
    return pl.pallas_call(
        functools.partial(gram_kernel, own),
        grid=(4,),
        out_shape=jax.ShapeDtypeStruct((NP // 2, SUB, ROWS, U), BF16),
        in_specs=[
            pl.BlockSpec((2, 8, A, U), lambda i: (0, i, 0, 0)),
            pl.BlockSpec((2, 8, A), lambda i: (0, i, 0)),
            pl.BlockSpec((2, 16, 32), lambda i: (0, 0, 0)),
        ],
        out_specs=pl.BlockSpec((1, SUB, ROWS, U), lambda i: (i, 0, 0, 0)),
        scratch_shapes=[pltpu.VMEM((4, 32, U), F32)],
        compiler_params=pltpu.CompilerParams(vmem_limit_bytes=8 << 20),
        cost_estimate=pl.CostEstimate(flops=3 * 10**8, bytes_accessed=3 << 20, transcendentals=0),
        name="gram_own" if own else "gram_mate",
    )(channel, received, cot)


def detect_kernel(noise_ref, count_ref, rx_ref, steps_ref, out_ref, gram_w, step_w):
    panel = lax.axis_index("panel")
    for k in range(3):
        w_re, w_im = steps_ref[k, 0], steps_ref[k, 1]
        re_hi, re_lo = split(w_re)
        im_hi, im_lo = split(w_im)
        for n, (re, im) in enumerate(((re_hi, im_hi), (re_lo, im_lo))):
            step_w[k, n, 0:U, 0:U] = re
            step_w[k, n, 0:U, U:] = -im
            step_w[k, n, U:, 0:U] = im
            step_w[k, n, U:, U:] = re
    row, col = iota((U, U), 0), iota((U, U), 1)
    at = iota((8, 2 * U), 0)
    at1 = iota((8, 1), 0)
    match = jnp.zeros((8, 2 * U), F32)
    cot = jnp.zeros((8, 2 * U), F32)
    for s in range(SUB):
        total = rx_ref[0, s].astype(F32)
        for p in range(1, NP // 2):
            total = total + rx_ref[p, s].astype(F32)
        tri = total[0:U]
        flip = tri.T
        g_re = jnp.where(row <= col, tri, flip)
        g_im = jnp.where(row > col, tri, jnp.where(row < col, -flip, 0.0))
        re_hi, re_lo = split(g_re)
        im_hi, im_lo = split(g_im)
        for n, (re, im) in enumerate(((re_hi, im_hi), (re_lo, im_lo))):
            gram_w[s, n, 0:U, 0:U] = re
            gram_w[s, n, 0:U, U:] = -im
            gram_w[s, n, U:, 0:U] = im
            gram_w[s, n, U:, U:] = re
        ext = total[U:ROWS]
        m_row = jnp.concatenate([ext[0:1] + ext[1:2], ext[2:3] + ext[3:4]], axis=1)
        c_row = jnp.concatenate([ext[4:5] + ext[5:6], ext[6:7] + ext[7:8]], axis=1)
        alive = (panel * SUB + s < count_ref[0]).astype(F32)
        match = jnp.where(at == s, jnp.broadcast_to(m_row, (8, 2 * U)), match)
        cot = jnp.where(at == s, jnp.broadcast_to(c_row * alive, (8, 2 * U)), cot)
    sigma = jnp.zeros((8, 1), F32)
    for s in range(SUB):
        sigma = jnp.where(at1 == s, noise_ref[panel * SUB + s], sigma)

    def parts(v):
        high, low = split(v)
        return jnp.concatenate([high, low], axis=0)

    def times_gram(v):
        both = parts(v)
        out = sigma * v
        for s in range(SUB):
            one = dot(both, gram_w[s, 0])
            two = dot(both, gram_w[s, 1])
            out = out + jnp.where(at == s, one[0:8] + one[8:16] + two[0:8], 0.0)
        return out

    def times_step(k, v, dims):
        both = parts(v)
        one = dot(both, step_w[k, 0], dims)
        two = dot(both, step_w[k, 1], dims)
        return one[0:8] + one[8:16] + two[0:8]

    def total_of(a, b):
        return jnp.sum(a * b, axis=1, keepdims=True)

    r = match
    energy = total_of(r, r) + EPS
    rs, ds, qs, es, al, cs, bs = [], [], [], [energy], [], [], []
    for k in range(3):
        d = r + times_step(k, r, NT)
        ratio = None
        if k > 0:
            ratio = es[k] / es[k - 1]
            d = d + ratio * ds[-1]
        q = times_gram(d)
        along = total_of(d, r)
        curve = total_of(d, q) + EPS
        alpha = along / curve
        rs.append(r)
        ds.append(d)
        qs.append(q)
        al.append(alpha)
        cs.append(curve)
        bs.append(ratio)
        if k < 2:
            r = r - alpha * q
            es.append(total_of(r, r) + EPS)

    qb, db = [None] * 3, [None] * 3
    rb = None
    d_next = None
    e_bar = [jnp.zeros((8, 1), F32) for _ in range(3)]
    for k in (2, 1, 0):
        a_bar = total_of(cot, ds[k])
        if rb is not None:
            a_bar = a_bar - total_of(rb, qs[k])
        along_bar = a_bar / cs[k]
        curve_bar = -along_bar * al[k]
        d_bar = al[k] * cot + along_bar * rs[k] + curve_bar * qs[k]
        if d_next is not None:
            d_bar = d_bar + d_next
        if rb is None:
            qb[k] = curve_bar * ds[k]
            d_bar = d_bar + curve_bar * qs[k]
            rb = along_bar * ds[k]
        else:
            qb[k] = curve_bar * ds[k] - al[k] * rb
            d_bar = d_bar + times_gram(qb[k])
            rb = rb + along_bar * ds[k]
        db[k] = d_bar
        rb = rb + d_bar + times_step(k, d_bar, NN)
        if k > 0:
            b_bar = total_of(d_bar, ds[k - 1]) / es[k - 1]
            e_bar[k] = e_bar[k] + b_bar
            e_bar[k - 1] = e_bar[k - 1] - b_bar * bs[k]
            d_next = bs[k] * d_bar
        rb = rb + 2.0 * e_bar[k] * rs[k]

    for s in range(SUB):
        block = rows_of([(v, s) for v in (qb[0], ds[0], qb[1], ds[1], qb[2], ds[2], rb)], 8)
        both = jnp.concatenate([block[:, 0:U], block[:, U:]], axis=0).astype(BF16)
        for p in range(NP):
            out_ref[p, 16 * s : 16 * s + 16, :] = both
    zeros = jnp.zeros((8, 2 * U), F32)
    for k in range(3):
        d_hi, d_lo = split(db[k])
        r_hi, r_lo = split(rs[k])
        left = jnp.concatenate([d_hi, d_lo, d_hi, zeros.astype(BF16)], axis=0)
        right = jnp.concatenate([r_hi, r_hi, r_lo, zeros.astype(BF16)], axis=0)
        outer = dot(left, right, TN)
        g_re = (outer[0:U, 0:U] + outer[U:, U:]).astype(BF16)
        g_im = (outer[U:, 0:U] - outer[0:U, U:]).astype(BF16)
        for p in range(NP):
            base = 64 + k * 32
            out_ref[p, base : base + 16, :] = g_re[16 * p : 16 * p + 16]
            out_ref[p, base + 16 : base + 32, :] = g_im[16 * p : 16 * p + 16]


def detect_call(noise, counts, rx, steps):
    smem = pl.BlockSpec(memory_space=pltpu.SMEM)
    vmem = pl.BlockSpec(memory_space=pltpu.VMEM)
    return pl.pallas_call(
        detect_kernel,
        out_shape=jax.ShapeDtypeStruct((NP, 160, U), BF16),
        in_specs=[smem, smem, vmem, vmem],
        out_specs=vmem,
        scratch_shapes=[
            pltpu.VMEM((SUB, 2, 2 * U, 2 * U), BF16),
            pltpu.VMEM((3, 2, 2 * U, 2 * U), BF16),
        ],
        compiler_params=pltpu.CompilerParams(vmem_limit_bytes=16 << 20),
        cost_estimate=pl.CostEstimate(flops=10**9, bytes_accessed=4 << 20, transcendentals=0),
        name="detect",
    )(noise, counts, rx, steps)


def chain_kernel(chan_ref, recv_ref, fac_ref, gchan_ref, grecv_ref):
    at = iota((8, U), 0)
    even = iota((16, U), 0) % 2 == 0
    gy_re = jnp.zeros((8, A), F32)
    gy_im = jnp.zeros((8, A), F32)
    y_re, y_im = recv_ref[0].astype(F32), recv_ref[1].astype(F32)
    for j in range(8):
        s = j % SUB
        fac = fac_ref[j // SUB, 16 * s : 16 * s + 16, :]
        chan = jnp.concatenate([chan_ref[0, j], chan_ref[1, j]], axis=0)
        prod = dot(fac, chan, NT)
        v_re = prod[0:8, 0:A] - prod[8:16, A:]
        v_im = prod[0:8, A:] + prod[8:16, 0:A]
        gy_re = jnp.where(at == j, jnp.broadcast_to(v_re[6:7], (8, A)), gy_re)
        gy_im = jnp.where(at == j, jnp.broadcast_to(v_im[6:7], (8, A)), gy_im)
        v_re = jnp.where(at == 7, jnp.broadcast_to(y_re[j : j + 1], (8, A)), v_re)
        v_im = jnp.where(at == 7, jnp.broadcast_to(y_im[j : j + 1], (8, A)), v_im)
        re_hi, re_lo = split(v_re)
        im_hi, im_lo = split(v_im)
        left = jnp.concatenate([re_hi, im_hi, re_lo, im_lo], axis=0)
        wide = fac.astype(F32)
        down = jnp.concatenate([wide[1:16], wide[0:1]], axis=0)
        up = jnp.concatenate([wide[15:16], wide[0:15]], axis=0)
        mate = jnp.where(even, down, up)
        g_re, g_im = mate[0:8], mate[8:16]
        right = jnp.concatenate(
            [jnp.concatenate([g_re, -g_im], axis=1), jnp.concatenate([g_im, g_re], axis=1)], axis=0
        ).astype(BF16)
        right = jnp.concatenate([right, right], axis=0)
        out = dot(left, right, TN)
        gchan_ref[0, j] = out[:, 0:U].astype(BF16)
        gchan_ref[1, j] = out[:, U:].astype(BF16)
    grecv_ref[0] = gy_re.astype(BF16)
    grecv_ref[1] = gy_im.astype(BF16)


def chain_call(channel, received, factors):
    return pl.pallas_call(
        chain_kernel,
        grid=(4,),
        out_shape=(
            jax.ShapeDtypeStruct((2, 32, A, U), BF16),
            jax.ShapeDtypeStruct((2, 32, A), BF16),
        ),
        in_specs=[
            pl.BlockSpec((2, 8, A, U), lambda i: (0, i, 0, 0)),
            pl.BlockSpec((2, 8, A), lambda i: (0, i, 0)),
            pl.BlockSpec((2, 64, U), lambda i: (i, 0, 0)),
        ],
        out_specs=(
            pl.BlockSpec((2, 8, A, U), lambda i: (0, i, 0, 0)),
            pl.BlockSpec((2, 8, A), lambda i: (0, i, 0)),
        ),
        compiler_params=pltpu.CompilerParams(vmem_limit_bytes=8 << 20),
        cost_estimate=pl.CostEstimate(flops=10**9, bytes_accessed=20 << 20, transcendentals=0),
        name="chain",
    )(channel, received, factors)


def widen_kernel(in_ref, out_ref):
    for p in range(NP):
        for k in range(6):
            rows = in_ref[p, 16 * k : 16 * k + 16, :].astype(F32)
            out_ref[k // 2, k % 2, 16 * p : 16 * p + 16, :] = rows


def widen_call(every):
    vmem = pl.BlockSpec(memory_space=pltpu.VMEM)
    return pl.pallas_call(
        widen_kernel,
        out_shape=jax.ShapeDtypeStruct((3, 2, U, U), F32),
        in_specs=[vmem],
        out_specs=vmem,
        compiler_params=pltpu.CompilerParams(vmem_limit_bytes=4 << 20),
        name="widen",
    )(every)


def exchange(value, axis, groups=None):
    return lax.all_to_all(
        value, axis, split_axis=0, concat_axis=0, tiled=True, axis_index_groups=groups
    )


def on_device(channel, received, noise, steps, cotangent, counts):
    z_groups = [[8 * z + y for z in range(8)] for y in range(8)]
    y_groups = [[8 * z + y for y in range(8)] for z in range(8)]
    cot = jnp.swapaxes(cotangent, 1, 2)
    away = gram_call(False, channel, received, cot)
    got = lax.ppermute(away, "panel", [(p, p ^ 1) for p in range(NP)])
    own = gram_call(True, channel, received, cot)
    pair = (own.astype(F32) + got.astype(F32)).astype(BF16)
    rx = exchange(pair, "panel", [[0, 2, 4, 6], [1, 3, 5, 7]])
    both = exchange(detect_call(noise, counts, rx, steps), "panel")
    part = jnp.sum(both[:, 64:].astype(F32), axis=0).astype(BF16)
    grad_channel, grad_received = chain_call(channel, received, both)
    for groups in (y_groups, z_groups):
        every = exchange(jnp.broadcast_to(part, (8, 96, U)), "sc", groups)
        part = jnp.sum(every.astype(F32), axis=0).astype(BF16)
    part, grad_received = lax.optimization_barrier((part, grad_received))
    every = exchange(jnp.broadcast_to(part, (8, 96, U)), "panel")
    return (grad_channel, grad_received, widen_call(every))


def solution(mesh):
    return jax.shard_map(
        on_device,
        mesh=mesh,
        in_specs=(
            P(None, "sc", "panel", None),
            P(None, "sc", "panel"),
            P("sc"),
            P(),
            P(None, "sc", "panel"),
            P("sc"),
        ),
        out_specs=(P(None, "sc", "panel", None), P(None, "sc", "panel"), P()),
        check_vma=False,
    )
```

```python
import functools

import jax
import jax.numpy as jnp
from jax import lax
from jax.experimental import pallas as pl
from jax.experimental.pallas import tpu as pltpu
from jax.sharding import PartitionSpec as P

EPS = 1e-06
F32 = jnp.float32
BF16 = jnp.bfloat16
NP = 8
SUB = 4
U = 128
A = 128
ROWS = 144
NN = (((1,), (0,)), ((), ()))
NT = (((1,), (1,)), ((), ()))
TN = (((0,), (0,)), ((), ()))


def dot(left, right, dims=NN):
    return lax.dot_general(left, right, dims, preferred_element_type=F32)


def split(value):
    high = value.astype(BF16)
    return high, (value - high.astype(F32)).astype(BF16)


def iota(shape, axis):
    return lax.broadcasted_iota(jnp.int32, shape, axis)


def rows_of(pieces, count):
    width = pieces[0][0].shape[1]
    at = iota((count, width), 0)
    out = jnp.zeros((count, width), F32)
    for k, (array, row) in enumerate(pieces):
        out = jnp.where(at == k, jnp.broadcast_to(array[row : row + 1], (count, width)), out)
    return out


def gram_kernel(own, chan_ref, recv_ref, cot_ref, out_ref, cot_rows):
    panel = lax.axis_index("panel")
    step = pl.program_id(0)
    core = lax.rem(panel + (0 if own else 1), 2)

    @pl.when(step == 0)
    def _():
        place = (iota((16, U), 1) == panel * 16 + iota((16, U), 0)).astype(F32).astype(BF16)
        for part in range(2):
            high, low = split(cot_ref[part])
            cot_rows[2 * part] = dot(high, place, TN)
            cot_rows[2 * part + 1] = dot(low, place, TN)

    y_rows = jnp.concatenate([recv_ref[0], recv_ref[1]], axis=1)
    y_rows = jnp.concatenate([y_rows, jnp.zeros_like(y_rows)], axis=0)
    upper = iota((U, U), 0) <= iota((U, U), 1)
    at = iota((8, 2 * U), 0)
    for j in range(SUB):
        row = core * SUB + j
        h_re, h_im = chan_ref[0, j], chan_ref[1, j]
        stack = jnp.concatenate([h_re, h_im], axis=0)
        other = jnp.concatenate([h_im, -h_re], axis=0)
        both = jnp.concatenate([stack, other], axis=1)
        left = jnp.concatenate([stack.T, y_rows], axis=0)
        prod = dot(left, both)
        packed = jnp.where(upper, prod[:U, :U], prod[:U, U:])
        match = jnp.sum(jnp.where(at == row, prod[U : U + 8], 0.0), axis=0, keepdims=True)
        m_re, m_im = match[:, :U], -match[:, U:]
        m_re_high, m_im_high = m_re.astype(BF16).astype(F32), m_im.astype(BF16).astype(F32)
        extra = rows_of(
            [(m_re_high, 0), (m_re - m_re_high, 0), (m_im_high, 0), (m_im - m_im_high, 0)]
            + [(cot_rows[k, pl.ds(step * 8 + row, 1), :], 0) for k in range(4)],
            16,
        )
        out_ref[0, j, 0:U, :] = packed.astype(BF16)
        out_ref[0, j, U:ROWS, :] = extra.astype(BF16)


def gram_call(own, channel, received, cot):
    def place(i):
        core = lax.rem(lax.axis_index("panel") + (0 if own else 1), 2)
        return (0, 2 * i + core, 0, 0)

    return pl.pallas_call(
        functools.partial(gram_kernel, own),
        grid=(4,),
        out_shape=jax.ShapeDtypeStruct((NP // 2, SUB, ROWS, U), BF16),
        in_specs=[
            pl.BlockSpec((2, SUB, A, U), place),
            pl.BlockSpec((2, 8, A), lambda i: (0, i, 0)),
            pl.BlockSpec((2, 16, 32), lambda i: (0, 0, 0)),
        ],
        out_specs=pl.BlockSpec((1, SUB, ROWS, U), lambda i: (i, 0, 0, 0)),
        scratch_shapes=[pltpu.VMEM((4, 32, U), F32)],
        cost_estimate=pl.CostEstimate(flops=3 * 10**8, bytes_accessed=3 << 20, transcendentals=0),
        name="gram_own" if own else "gram_mate",
    )(channel, received, cot)


def detect_kernel(noise_ref, count_ref, rx_ref, steps_ref, out_ref, gram_w, step_w):
    panel = lax.axis_index("panel")
    for k in range(3):
        w_re, w_im = steps_ref[k, 0], steps_ref[k, 1]
        re_hi, re_lo = split(w_re)
        im_hi, im_lo = split(w_im)
        for n, (re, im) in enumerate(((re_hi, im_hi), (re_lo, im_lo))):
            step_w[k, n, 0:U, 0:U] = re
            step_w[k, n, 0:U, U:] = -im
            step_w[k, n, U:, 0:U] = im
            step_w[k, n, U:, U:] = re
    row, col = iota((U, U), 0), iota((U, U), 1)
    at = iota((8, 2 * U), 0)
    at1 = iota((8, 1), 0)
    match = jnp.zeros((8, 2 * U), F32)
    cot = jnp.zeros((8, 2 * U), F32)
    for s in range(SUB):
        total = rx_ref[0, s].astype(F32)
        for p in range(1, NP // 2):
            total = total + rx_ref[p, s].astype(F32)
        tri = total[0:U]
        flip = tri.T
        g_re = jnp.where(row <= col, tri, flip)
        g_im = jnp.where(row > col, tri, jnp.where(row < col, -flip, 0.0))
        re_hi, re_lo = split(g_re)
        im_hi, im_lo = split(g_im)
        for n, (re, im) in enumerate(((re_hi, im_hi), (re_lo, im_lo))):
            gram_w[s, n, 0:U, 0:U] = re
            gram_w[s, n, 0:U, U:] = -im
            gram_w[s, n, U:, 0:U] = im
            gram_w[s, n, U:, U:] = re
        ext = total[U:ROWS]
        m_row = jnp.concatenate([ext[0:1] + ext[1:2], ext[2:3] + ext[3:4]], axis=1)
        c_row = jnp.concatenate([ext[4:5] + ext[5:6], ext[6:7] + ext[7:8]], axis=1)
        alive = (panel * SUB + s < count_ref[0]).astype(F32)
        match = jnp.where(at == s, jnp.broadcast_to(m_row, (8, 2 * U)), match)
        cot = jnp.where(at == s, jnp.broadcast_to(c_row * alive, (8, 2 * U)), cot)
    sigma = jnp.zeros((8, 1), F32)
    for s in range(SUB):
        sigma = jnp.where(at1 == s, noise_ref[panel * SUB + s], sigma)

    def parts(v):
        high, low = split(v)
        return jnp.concatenate([high, low], axis=0)

    def times_gram(v):
        both = parts(v)
        out = sigma * v
        for s in range(SUB):
            one = dot(both, gram_w[s, 0])
            two = dot(both, gram_w[s, 1])
            out = out + jnp.where(at == s, one[0:8] + one[8:16] + two[0:8], 0.0)
        return out

    def times_step(k, v, dims):
        both = parts(v)
        one = dot(both, step_w[k, 0], dims)
        two = dot(both, step_w[k, 1], dims)
        return one[0:8] + one[8:16] + two[0:8]

    def total_of(a, b):
        return jnp.sum(a * b, axis=1, keepdims=True)

    r = match
    energy = total_of(r, r) + EPS
    rs, ds, qs, es, al, cs, bs = [], [], [], [energy], [], [], []
    for k in range(3):
        d = r + times_step(k, r, NT)
        ratio = None
        if k > 0:
            ratio = es[k] / es[k - 1]
            d = d + ratio * ds[-1]
        q = times_gram(d)
        along = total_of(d, r)
        curve = total_of(d, q) + EPS
        alpha = along / curve
        rs.append(r)
        ds.append(d)
        qs.append(q)
        al.append(alpha)
        cs.append(curve)
        bs.append(ratio)
        if k < 2:
            r = r - alpha * q
            es.append(total_of(r, r) + EPS)

    qb, db = [None] * 3, [None] * 3
    rb = None
    d_next = None
    e_bar = [jnp.zeros((8, 1), F32) for _ in range(3)]
    for k in (2, 1, 0):
        a_bar = total_of(cot, ds[k])
        if rb is not None:
            a_bar = a_bar - total_of(rb, qs[k])
        along_bar = a_bar / cs[k]
        curve_bar = -along_bar * al[k]
        d_bar = al[k] * cot + along_bar * rs[k] + curve_bar * qs[k]
        if d_next is not None:
            d_bar = d_bar + d_next
        if rb is None:
            qb[k] = curve_bar * ds[k]
            d_bar = d_bar + curve_bar * qs[k]
            rb = along_bar * ds[k]
        else:
            qb[k] = curve_bar * ds[k] - al[k] * rb
            d_bar = d_bar + times_gram(qb[k])
            rb = rb + along_bar * ds[k]
        db[k] = d_bar
        rb = rb + d_bar + times_step(k, d_bar, NN)
        if k > 0:
            b_bar = total_of(d_bar, ds[k - 1]) / es[k - 1]
            e_bar[k] = e_bar[k] + b_bar
            e_bar[k - 1] = e_bar[k - 1] - b_bar * bs[k]
            d_next = bs[k] * d_bar
        rb = rb + 2.0 * e_bar[k] * rs[k]

    for s in range(SUB):
        block = rows_of([(v, s) for v in (qb[0], ds[0], qb[1], ds[1], qb[2], ds[2], rb)], 8)
        both = jnp.concatenate([block[:, 0:U], block[:, U:]], axis=0).astype(BF16)
        for p in range(NP):
            out_ref[p, 16 * s : 16 * s + 16, :] = both
    zeros = jnp.zeros((8, 2 * U), F32)
    for k in range(3):
        d_hi, d_lo = split(db[k])
        r_hi, r_lo = split(rs[k])
        left = jnp.concatenate([d_hi, d_lo, d_hi, zeros.astype(BF16)], axis=0)
        right = jnp.concatenate([r_hi, r_hi, r_lo, zeros.astype(BF16)], axis=0)
        outer = dot(left, right, TN)
        g_re = (outer[0:U, 0:U] + outer[U:, U:]).astype(BF16)
        g_im = (outer[U:, 0:U] - outer[0:U, U:]).astype(BF16)
        for p in range(NP):
            base = 64 + k * 32
            out_ref[p, base : base + 16, :] = g_re[16 * p : 16 * p + 16]
            out_ref[p, base + 16 : base + 32, :] = g_im[16 * p : 16 * p + 16]


def detect_call(noise, counts, rx, steps):
    smem = pl.BlockSpec(memory_space=pltpu.SMEM)
    vmem = pl.BlockSpec(memory_space=pltpu.VMEM)
    return pl.pallas_call(
        detect_kernel,
        out_shape=jax.ShapeDtypeStruct((NP, 160, U), BF16),
        in_specs=[smem, smem, vmem, vmem],
        out_specs=vmem,
        scratch_shapes=[
            pltpu.VMEM((SUB, 2, 2 * U, 2 * U), BF16),
            pltpu.VMEM((3, 2, 2 * U, 2 * U), BF16),
        ],
        compiler_params=pltpu.CompilerParams(vmem_limit_bytes=16 << 20),
        cost_estimate=pl.CostEstimate(flops=10**9, bytes_accessed=4 << 20, transcendentals=0),
        name="detect",
    )(noise, counts, rx, steps)


def chain_kernel(chan_ref, recv_ref, fac_ref, *rest):
    gchan_ref, grecv_ref = rest[-2:]
    at = iota((8, U), 0)
    even = iota((16, U), 0) % 2 == 0
    gy_re = jnp.zeros((8, A), F32)
    gy_im = jnp.zeros((8, A), F32)
    y_re, y_im = recv_ref[0].astype(F32), recv_ref[1].astype(F32)
    for j in range(8):
        s = j % SUB
        fac = fac_ref[j // SUB, 16 * s : 16 * s + 16, :]
        chan = jnp.concatenate([chan_ref[0, j], chan_ref[1, j]], axis=0)
        prod = dot(fac, chan, NT)
        v_re = prod[0:8, 0:A] - prod[8:16, A:]
        v_im = prod[0:8, A:] + prod[8:16, 0:A]
        gy_re = jnp.where(at == j, jnp.broadcast_to(v_re[6:7], (8, A)), gy_re)
        gy_im = jnp.where(at == j, jnp.broadcast_to(v_im[6:7], (8, A)), gy_im)
        v_re = jnp.where(at == 7, jnp.broadcast_to(y_re[j : j + 1], (8, A)), v_re)
        v_im = jnp.where(at == 7, jnp.broadcast_to(y_im[j : j + 1], (8, A)), v_im)
        re_hi, re_lo = split(v_re)
        im_hi, im_lo = split(v_im)
        left = jnp.concatenate([re_hi, im_hi, re_lo, im_lo], axis=0)
        wide = fac.astype(F32)
        down = jnp.concatenate([wide[1:16], wide[0:1]], axis=0)
        up = jnp.concatenate([wide[15:16], wide[0:15]], axis=0)
        mate = jnp.where(even, down, up)
        g_re, g_im = mate[0:8], mate[8:16]
        right = jnp.concatenate(
            [jnp.concatenate([g_re, -g_im], axis=1), jnp.concatenate([g_im, g_re], axis=1)], axis=0
        ).astype(BF16)
        right = jnp.concatenate([right, right], axis=0)
        out = dot(left, right, TN)
        gchan_ref[0, j] = out[:, 0:U].astype(BF16)
        gchan_ref[1, j] = out[:, U:].astype(BF16)
    grecv_ref[0] = gy_re.astype(BF16)
    grecv_ref[1] = gy_im.astype(BF16)


def chain_call(half, channel, received, factors, earlier=()):
    wide = pl.BlockSpec((2, 8, A, U), lambda i: (0, i + 2 * half, 0, 0))
    flat = pl.BlockSpec((2, 8, A), lambda i: (0, i + 2 * half, 0))
    return pl.pallas_call(
        chain_kernel,
        grid=(2,),
        out_shape=(
            jax.ShapeDtypeStruct((2, 32, A, U), BF16),
            jax.ShapeDtypeStruct((2, 32, A), BF16),
        ),
        in_specs=[wide, flat, pl.BlockSpec((2, 64, U), lambda i: (i + 2 * half, 0, 0))]
        + [pl.BlockSpec(memory_space=pl.ANY)] * len(earlier),
        out_specs=(wide, flat),
        input_output_aliases={3: 0, 4: 1} if earlier else {},
        compiler_params=pltpu.CompilerParams(vmem_limit_bytes=8 << 20),
        cost_estimate=pl.CostEstimate(flops=10**9, bytes_accessed=12 << 20, transcendentals=0),
        name="chain_b" if earlier else "chain_a",
    )(channel, received, factors, *earlier)


def widen_kernel(in_ref, out_ref):
    for p in range(NP):
        for k in range(6):
            rows = in_ref[p, 16 * k : 16 * k + 16, :].astype(F32)
            out_ref[k // 2, k % 2, 16 * p : 16 * p + 16, :] = rows


def widen_call(every):
    vmem = pl.BlockSpec(memory_space=pltpu.VMEM)
    return pl.pallas_call(
        widen_kernel,
        out_shape=jax.ShapeDtypeStruct((3, 2, U, U), F32),
        in_specs=[vmem],
        out_specs=vmem,
        compiler_params=pltpu.CompilerParams(vmem_limit_bytes=4 << 20),
        name="widen",
    )(every)


def exchange(value, axis, groups=None):
    return lax.all_to_all(
        value, axis, split_axis=0, concat_axis=0, tiled=True, axis_index_groups=groups
    )


def on_device(channel, received, noise, steps, cotangent, counts):
    z_groups = [[8 * z + y for z in range(8)] for y in range(8)]
    y_groups = [[8 * z + y for y in range(8)] for z in range(8)]
    cot = jnp.swapaxes(cotangent, 1, 2)
    away = gram_call(False, channel, received, cot)
    got = lax.ppermute(away, "panel", [(p, p ^ 1) for p in range(NP)])
    own = gram_call(True, channel, received, cot)
    pair = (own.astype(F32) + got.astype(F32)).astype(BF16)
    rx = exchange(pair, "panel", [[0, 2, 4, 6], [1, 3, 5, 7]])
    both = exchange(detect_call(noise, counts, rx, steps), "panel")
    part = jnp.sum(both[:, 64:].astype(F32), axis=0).astype(BF16)
    grads = ()
    for half, groups in enumerate((y_groups, z_groups)):
        grads = chain_call(half, channel, received, both, grads)
        every = exchange(jnp.broadcast_to(part, (8, 96, U)), "sc", groups)
        part = jnp.sum(every.astype(F32), axis=0).astype(BF16)
        part, grads = lax.optimization_barrier((part, grads))
    grad_channel, grad_received = grads
    every = exchange(jnp.broadcast_to(part, (8, 96, U)), "panel")
    return (grad_channel, grad_received, widen_call(every))


def solution(mesh):
    return jax.shard_map(
        on_device,
        mesh=mesh,
        in_specs=(
            P(None, "sc", "panel", None),
            P(None, "sc", "panel"),
            P("sc"),
            P(),
            P(None, "sc", "panel"),
            P("sc"),
        ),
        out_specs=(P(None, "sc", "panel", None), P(None, "sc", "panel"), P()),
        check_vma=False,
    )
```

```python
import functools

import jax
import jax.numpy as jnp
from jax import lax
from jax.experimental import pallas as pl
from jax.experimental.pallas import tpu as pltpu
from jax.sharding import PartitionSpec as P

EPS = 1e-06
F32 = jnp.float32
BF16 = jnp.bfloat16
NP = 8
SUB = 4
U = 128
A = 128
ROWS = 144
NN = (((1,), (0,)), ((), ()))
NT = (((1,), (1,)), ((), ()))
TN = (((0,), (0,)), ((), ()))


def dot(left, right, dims=NN):
    return lax.dot_general(left, right, dims, preferred_element_type=F32)


def split(value):
    high = value.astype(BF16)
    return high, (value - high.astype(F32)).astype(BF16)


def iota(shape, axis):
    return lax.broadcasted_iota(jnp.int32, shape, axis)


def rows_of(pieces, count):
    width = pieces[0][0].shape[1]
    at = iota((count, width), 0)
    out = jnp.zeros((count, width), F32)
    for k, (array, row) in enumerate(pieces):
        out = jnp.where(at == k, jnp.broadcast_to(array[row : row + 1], (count, width)), out)
    return out


def gram_kernel(own, chan_ref, recv_ref, cot_ref, out_ref, cot_rows):
    panel = lax.axis_index("panel")
    step = pl.program_id(0)
    core = lax.rem(panel + (0 if own else 1), 2)

    @pl.when(step == 0)
    def _():
        place = (iota((16, U), 1) == panel * 16 + iota((16, U), 0)).astype(F32).astype(BF16)
        for part in range(2):
            high, low = split(cot_ref[part])
            cot_rows[2 * part] = dot(high, place, TN)
            cot_rows[2 * part + 1] = dot(low, place, TN)

    y_rows = jnp.concatenate([recv_ref[0], recv_ref[1]], axis=1)
    y_rows = jnp.concatenate([y_rows, jnp.zeros_like(y_rows)], axis=0)
    upper = iota((U, U), 0) <= iota((U, U), 1)
    at = iota((8, 2 * U), 0)
    for j in range(SUB):
        row = core * SUB + j
        h_re, h_im = chan_ref[0, row], chan_ref[1, row]
        stack = jnp.concatenate([h_re, h_im], axis=0)
        other = jnp.concatenate([h_im, -h_re], axis=0)
        both = jnp.concatenate([stack, other], axis=1)
        left = jnp.concatenate([stack.T, y_rows], axis=0)
        prod = dot(left, both)
        packed = jnp.where(upper, prod[:U, :U], prod[:U, U:])
        match = jnp.sum(jnp.where(at == row, prod[U : U + 8], 0.0), axis=0, keepdims=True)
        m_re, m_im = match[:, :U], -match[:, U:]
        m_re_high, m_im_high = m_re.astype(BF16).astype(F32), m_im.astype(BF16).astype(F32)
        extra = rows_of(
            [(m_re_high, 0), (m_re - m_re_high, 0), (m_im_high, 0), (m_im - m_im_high, 0)]
            + [(cot_rows[k, pl.ds(step * 8 + row, 1), :], 0) for k in range(4)],
            16,
        )
        out_ref[0, j, 0:U, :] = packed.astype(BF16)
        out_ref[0, j, U:ROWS, :] = extra.astype(BF16)


def gram_call(own, channel, received, cot):
    return pl.pallas_call(
        functools.partial(gram_kernel, own),
        grid=(4,),
        out_shape=jax.ShapeDtypeStruct((NP // 2, SUB, ROWS, U), BF16),
        in_specs=[
            pl.BlockSpec((2, 8, A, U), lambda i: (0, i, 0, 0)),
            pl.BlockSpec((2, 8, A), lambda i: (0, i, 0)),
            pl.BlockSpec((2, 16, 32), lambda i: (0, 0, 0)),
        ],
        out_specs=pl.BlockSpec((1, SUB, ROWS, U), lambda i: (i, 0, 0, 0)),
        scratch_shapes=[pltpu.VMEM((4, 32, U), F32)],
        compiler_params=pltpu.CompilerParams(vmem_limit_bytes=8 << 20),
        cost_estimate=pl.CostEstimate(flops=3 * 10**8, bytes_accessed=3 << 20, transcendentals=0),
        name="gram_own" if own else "gram_mate",
    )(channel, received, cot)


def detect_kernel(noise_ref, count_ref, rx_ref, steps_ref, out_ref, gram_w, step_w):
    panel = lax.axis_index("panel")
    for k in range(3):
        w_re, w_im = steps_ref[k, 0], steps_ref[k, 1]
        re_hi, re_lo = split(w_re)
        im_hi, im_lo = split(w_im)
        for n, (re, im) in enumerate(((re_hi, im_hi), (re_lo, im_lo))):
            step_w[k, n, 0:U, 0:U] = re
            step_w[k, n, 0:U, U:] = -im
            step_w[k, n, U:, 0:U] = im
            step_w[k, n, U:, U:] = re
    row, col = iota((U, U), 0), iota((U, U), 1)
    at = iota((8, 2 * U), 0)
    at1 = iota((8, 1), 0)
    match = jnp.zeros((8, 2 * U), F32)
    cot = jnp.zeros((8, 2 * U), F32)
    for s in range(SUB):
        total = rx_ref[0, s].astype(F32)
        for p in range(1, NP // 2):
            total = total + rx_ref[p, s].astype(F32)
        tri = total[0:U]
        flip = tri.T
        g_re = jnp.where(row <= col, tri, flip)
        g_im = jnp.where(row > col, tri, jnp.where(row < col, -flip, 0.0))
        re_hi, re_lo = split(g_re)
        im_hi, im_lo = split(g_im)
        for n, (re, im) in enumerate(((re_hi, im_hi), (re_lo, im_lo))):
            gram_w[s, n, 0:U, 0:U] = re
            gram_w[s, n, 0:U, U:] = -im
            gram_w[s, n, U:, 0:U] = im
            gram_w[s, n, U:, U:] = re
        ext = total[U:ROWS]
        m_row = jnp.concatenate([ext[0:1] + ext[1:2], ext[2:3] + ext[3:4]], axis=1)
        c_row = jnp.concatenate([ext[4:5] + ext[5:6], ext[6:7] + ext[7:8]], axis=1)
        alive = (panel * SUB + s < count_ref[0]).astype(F32)
        match = jnp.where(at == s, jnp.broadcast_to(m_row, (8, 2 * U)), match)
        cot = jnp.where(at == s, jnp.broadcast_to(c_row * alive, (8, 2 * U)), cot)
    sigma = jnp.zeros((8, 1), F32)
    for s in range(SUB):
        sigma = jnp.where(at1 == s, noise_ref[panel * SUB + s], sigma)

    def parts(v):
        high, low = split(v)
        return jnp.concatenate([high, low], axis=0)

    def times_gram(v):
        both = parts(v)
        out = sigma * v
        for s in range(SUB):
            one = dot(both, gram_w[s, 0])
            two = dot(both, gram_w[s, 1])
            out = out + jnp.where(at == s, one[0:8] + one[8:16] + two[0:8], 0.0)
        return out

    def times_step(k, v, dims):
        both = parts(v)
        one = dot(both, step_w[k, 0], dims)
        two = dot(both, step_w[k, 1], dims)
        return one[0:8] + one[8:16] + two[0:8]

    def total_of(a, b):
        return jnp.sum(a * b, axis=1, keepdims=True)

    r = match
    energy = total_of(r, r) + EPS
    rs, ds, qs, es, al, cs, bs = [], [], [], [energy], [], [], []
    for k in range(3):
        d = r + times_step(k, r, NT)
        ratio = None
        if k > 0:
            ratio = es[k] / es[k - 1]
            d = d + ratio * ds[-1]
        q = times_gram(d)
        along = total_of(d, r)
        curve = total_of(d, q) + EPS
        alpha = along / curve
        rs.append(r)
        ds.append(d)
        qs.append(q)
        al.append(alpha)
        cs.append(curve)
        bs.append(ratio)
        if k < 2:
            r = r - alpha * q
            es.append(total_of(r, r) + EPS)

    qb, db = [None] * 3, [None] * 3
    rb = None
    d_next = None
    e_bar = [jnp.zeros((8, 1), F32) for _ in range(3)]
    for k in (2, 1, 0):
        a_bar = total_of(cot, ds[k])
        if rb is not None:
            a_bar = a_bar - total_of(rb, qs[k])
        along_bar = a_bar / cs[k]
        curve_bar = -along_bar * al[k]
        d_bar = al[k] * cot + along_bar * rs[k] + curve_bar * qs[k]
        if d_next is not None:
            d_bar = d_bar + d_next
        if rb is None:
            qb[k] = curve_bar * ds[k]
            d_bar = d_bar + curve_bar * qs[k]
            rb = along_bar * ds[k]
        else:
            qb[k] = curve_bar * ds[k] - al[k] * rb
            d_bar = d_bar + times_gram(qb[k])
            rb = rb + along_bar * ds[k]
        db[k] = d_bar
        rb = rb + d_bar + times_step(k, d_bar, NN)
        if k > 0:
            b_bar = total_of(d_bar, ds[k - 1]) / es[k - 1]
            e_bar[k] = e_bar[k] + b_bar
            e_bar[k - 1] = e_bar[k - 1] - b_bar * bs[k]
            d_next = bs[k] * d_bar
        rb = rb + 2.0 * e_bar[k] * rs[k]

    for s in range(SUB):
        block = rows_of([(v, s) for v in (qb[0], ds[0], qb[1], ds[1], qb[2], ds[2], rb)], 8)
        both = jnp.concatenate([block[:, 0:U], block[:, U:]], axis=0).astype(BF16)
        for p in range(NP):
            out_ref[p, 16 * s : 16 * s + 16, :] = both
    zeros = jnp.zeros((8, 2 * U), F32)
    for k in range(3):
        d_hi, d_lo = split(db[k])
        r_hi, r_lo = split(rs[k])
        left = jnp.concatenate([d_hi, d_lo, d_hi, zeros.astype(BF16)], axis=0)
        right = jnp.concatenate([r_hi, r_hi, r_lo, zeros.astype(BF16)], axis=0)
        outer = dot(left, right, TN)
        g_re = (outer[0:U, 0:U] + outer[U:, U:]).astype(BF16)
        g_im = (outer[U:, 0:U] - outer[0:U, U:]).astype(BF16)
        for p in range(NP):
            base = 64 + k * 32
            out_ref[p, base : base + 16, :] = g_re[16 * p : 16 * p + 16]
            out_ref[p, base + 16 : base + 32, :] = g_im[16 * p : 16 * p + 16]


def detect_call(noise, counts, rx, steps):
    smem = pl.BlockSpec(memory_space=pltpu.SMEM)
    vmem = pl.BlockSpec(memory_space=pltpu.VMEM)
    return pl.pallas_call(
        detect_kernel,
        out_shape=jax.ShapeDtypeStruct((NP, 160, U), BF16),
        in_specs=[smem, smem, vmem, vmem],
        out_specs=vmem,
        scratch_shapes=[
            pltpu.VMEM((SUB, 2, 2 * U, 2 * U), BF16),
            pltpu.VMEM((3, 2, 2 * U, 2 * U), BF16),
        ],
        compiler_params=pltpu.CompilerParams(vmem_limit_bytes=16 << 20),
        cost_estimate=pl.CostEstimate(flops=10**9, bytes_accessed=4 << 20, transcendentals=0),
        name="detect",
    )(noise, counts, rx, steps)


def chain_kernel(chan_ref, recv_ref, fac_ref, *rest):
    gchan_ref, grecv_ref = rest[-2:]
    at = iota((8, U), 0)
    even = iota((16, U), 0) % 2 == 0
    gy_re = jnp.zeros((8, A), F32)
    gy_im = jnp.zeros((8, A), F32)
    y_re, y_im = recv_ref[0].astype(F32), recv_ref[1].astype(F32)
    for j in range(8):
        s = j % SUB
        fac = fac_ref[j // SUB, 16 * s : 16 * s + 16, :]
        chan = jnp.concatenate([chan_ref[0, j], chan_ref[1, j]], axis=0)
        prod = dot(fac, chan, NT)
        v_re = prod[0:8, 0:A] - prod[8:16, A:]
        v_im = prod[0:8, A:] + prod[8:16, 0:A]
        gy_re = jnp.where(at == j, jnp.broadcast_to(v_re[6:7], (8, A)), gy_re)
        gy_im = jnp.where(at == j, jnp.broadcast_to(v_im[6:7], (8, A)), gy_im)
        v_re = jnp.where(at == 7, jnp.broadcast_to(y_re[j : j + 1], (8, A)), v_re)
        v_im = jnp.where(at == 7, jnp.broadcast_to(y_im[j : j + 1], (8, A)), v_im)
        re_hi, re_lo = split(v_re)
        im_hi, im_lo = split(v_im)
        left = jnp.concatenate([re_hi, im_hi, re_lo, im_lo], axis=0)
        wide = fac.astype(F32)
        down = jnp.concatenate([wide[1:16], wide[0:1]], axis=0)
        up = jnp.concatenate([wide[15:16], wide[0:15]], axis=0)
        mate = jnp.where(even, down, up)
        g_re, g_im = mate[0:8], mate[8:16]
        right = jnp.concatenate(
            [jnp.concatenate([g_re, -g_im], axis=1), jnp.concatenate([g_im, g_re], axis=1)], axis=0
        ).astype(BF16)
        right = jnp.concatenate([right, right], axis=0)
        out = dot(left, right, TN)
        gchan_ref[0, j] = out[:, 0:U].astype(BF16)
        gchan_ref[1, j] = out[:, U:].astype(BF16)
    grecv_ref[0] = gy_re.astype(BF16)
    grecv_ref[1] = gy_im.astype(BF16)


def chain_call(half, channel, received, factors, earlier=()):
    wide = pl.BlockSpec((2, 8, A, U), lambda i: (0, i + 2 * half, 0, 0))
    flat = pl.BlockSpec((2, 8, A), lambda i: (0, i + 2 * half, 0))
    return pl.pallas_call(
        chain_kernel,
        grid=(2,),
        out_shape=(
            jax.ShapeDtypeStruct((2, 32, A, U), BF16),
            jax.ShapeDtypeStruct((2, 32, A), BF16),
        ),
        in_specs=[wide, flat, pl.BlockSpec((2, 64, U), lambda i: (i + 2 * half, 0, 0))]
        + [pl.BlockSpec(memory_space=pl.ANY)] * len(earlier),
        out_specs=(wide, flat),
        input_output_aliases={3: 0, 4: 1} if earlier else {},
        compiler_params=pltpu.CompilerParams(vmem_limit_bytes=8 << 20),
        cost_estimate=pl.CostEstimate(flops=10**9, bytes_accessed=12 << 20, transcendentals=0),
        name="chain_b" if earlier else "chain_a",
    )(channel, received, factors, *earlier)


def widen_kernel(in_ref, out_ref):
    for p in range(NP):
        for k in range(6):
            rows = in_ref[p, 16 * k : 16 * k + 16, :].astype(F32)
            out_ref[k // 2, k % 2, 16 * p : 16 * p + 16, :] = rows


def widen_call(every):
    vmem = pl.BlockSpec(memory_space=pltpu.VMEM)
    return pl.pallas_call(
        widen_kernel,
        out_shape=jax.ShapeDtypeStruct((3, 2, U, U), F32),
        in_specs=[vmem],
        out_specs=vmem,
        compiler_params=pltpu.CompilerParams(vmem_limit_bytes=4 << 20),
        name="widen",
    )(every)


def exchange(value, axis, groups=None):
    return lax.all_to_all(
        value, axis, split_axis=0, concat_axis=0, tiled=True, axis_index_groups=groups
    )


def on_device(channel, received, noise, steps, cotangent, counts):
    z_groups = [[8 * z + y for z in range(8)] for y in range(8)]
    y_groups = [[8 * z + y for y in range(8)] for z in range(8)]
    cot = jnp.swapaxes(cotangent, 1, 2)
    away = gram_call(False, channel, received, cot)
    got = lax.ppermute(away, "panel", [(p, p ^ 1) for p in range(NP)])
    own = gram_call(True, channel, received, cot)
    pair = (own.astype(F32) + got.astype(F32)).astype(BF16)
    rx = exchange(pair, "panel", [[0, 2, 4, 6], [1, 3, 5, 7]])
    both = exchange(detect_call(noise, counts, rx, steps), "panel")
    part = jnp.sum(both[:, 64:].astype(F32), axis=0).astype(BF16)
    grads = ()
    for half, groups in enumerate((y_groups, z_groups)):
        grads = chain_call(half, channel, received, both, grads)
        every = exchange(jnp.broadcast_to(part, (8, 96, U)), "sc", groups)
        part = jnp.sum(every.astype(F32), axis=0).astype(BF16)
        part, grads = lax.optimization_barrier((part, grads))
    grad_channel, grad_received = grads
    every = exchange(jnp.broadcast_to(part, (8, 96, U)), "panel")
    return (grad_channel, grad_received, widen_call(every))


def solution(mesh):
    return jax.shard_map(
        on_device,
        mesh=mesh,
        in_specs=(
            P(None, "sc", "panel", None),
            P(None, "sc", "panel"),
            P("sc"),
            P(),
            P(None, "sc", "panel"),
            P("sc"),
        ),
        out_specs=(P(None, "sc", "panel", None), P(None, "sc", "panel"), P()),
        check_vma=False,
    )
```

```python
import functools

import jax
import jax.numpy as jnp
from jax import lax
from jax.experimental import pallas as pl
from jax.experimental.pallas import tpu as pltpu
from jax.sharding import PartitionSpec as P

EPS = 1e-06
F32 = jnp.float32
BF16 = jnp.bfloat16
NP = 8
SUB = 4
U = 128
A = 128
ROWS = 144
NN = (((1,), (0,)), ((), ()))
NT = (((1,), (1,)), ((), ()))
TN = (((0,), (0,)), ((), ()))


def dot(left, right, dims=NN):
    return lax.dot_general(left, right, dims, preferred_element_type=F32)


def split(value):
    high = value.astype(BF16)
    return high, (value - high.astype(F32)).astype(BF16)


def iota(shape, axis):
    return lax.broadcasted_iota(jnp.int32, shape, axis)


def rows_of(pieces, count):
    width = pieces[0][0].shape[1]
    at = iota((count, width), 0)
    out = jnp.zeros((count, width), F32)
    for k, (array, row) in enumerate(pieces):
        out = jnp.where(at == k, jnp.broadcast_to(array[row : row + 1], (count, width)), out)
    return out


def gram_kernel(own, chan_ref, recv_ref, cot_ref, out_ref, cot_rows):
    panel = lax.axis_index("panel")
    core = lax.rem(panel + (0 if own else 1), 2)

    place = (iota((16, U), 1) == panel * 16 + iota((16, U), 0)).astype(F32).astype(BF16)
    for part in range(2):
        high, low = split(cot_ref[part])
        cot_rows[2 * part] = dot(high, place, TN)
        cot_rows[2 * part + 1] = dot(low, place, TN)

    received = jnp.concatenate([recv_ref[0].astype(F32), recv_ref[1].astype(F32)], axis=1)
    upper = iota((U, U), 0) <= iota((U, U), 1)
    at = iota((8, 2 * U), 0)
    for step in range(4):
        y_rows = received[8 * step : 8 * step + 8]
        y_rows = jnp.concatenate([y_rows, jnp.zeros_like(y_rows)], axis=0).astype(BF16)
        for j in range(SUB):
            row = core * SUB + j
            h_re, h_im = chan_ref[0, step, 0, j], chan_ref[1, step, 0, j]
            stack = jnp.concatenate([h_re, h_im], axis=0)
            other = jnp.concatenate([h_im, -h_re], axis=0)
            both = jnp.concatenate([stack, other], axis=1)
            left = jnp.concatenate([stack.T, y_rows], axis=0)
            prod = dot(left, both)
            packed = jnp.where(upper, prod[:U, :U], prod[:U, U:])
            match = jnp.sum(jnp.where(at == row, prod[U : U + 8], 0.0), axis=0, keepdims=True)
            m_re, m_im = match[:, :U], -match[:, U:]
            m_re_high, m_im_high = m_re.astype(BF16).astype(F32), m_im.astype(BF16).astype(F32)
            extra = rows_of(
                [(m_re_high, 0), (m_re - m_re_high, 0), (m_im_high, 0), (m_im - m_im_high, 0)]
                + [(cot_rows[k, pl.ds(step * 8 + row, 1), :], 0) for k in range(4)],
                16,
            )
            out_ref[step, j, 0:U, :] = packed.astype(BF16)
            out_ref[step, j, U:ROWS, :] = extra.astype(BF16)


def gram_call(own, channel, received, cot):
    def place(i):
        return (0, 0, lax.rem(lax.axis_index("panel") + (0 if own else 1), 2), 0, 0, 0)

    limit = pltpu.CompilerParams(vmem_limit_bytes=8 << 20) if own else pltpu.CompilerParams()
    return pl.pallas_call(
        functools.partial(gram_kernel, own),
        grid=(1,),
        out_shape=jax.ShapeDtypeStruct((NP // 2, SUB, ROWS, U), BF16),
        in_specs=[
            pl.BlockSpec((2, 4, 1, SUB, A, U), place),
            pl.BlockSpec((2, 32, A), lambda i: (0, 0, 0)),
            pl.BlockSpec((2, 16, 32), lambda i: (0, 0, 0)),
        ],
        out_specs=pl.BlockSpec((NP // 2, SUB, ROWS, U), lambda i: (0, 0, 0, 0)),
        scratch_shapes=[pltpu.VMEM((4, 32, U), F32)],
        compiler_params=limit,
        cost_estimate=pl.CostEstimate(flops=3 * 10**8, bytes_accessed=3 << 20, transcendentals=0),
        name="gram_own" if own else "gram_mate",
    )(channel.reshape(2, 4, 2, SUB, A, U), received, cot)


def detect_kernel(noise_ref, count_ref, rx_ref, steps_ref, out_ref, gram_w, step_w):
    panel = lax.axis_index("panel")
    for k in range(3):
        w_re, w_im = steps_ref[k, 0], steps_ref[k, 1]
        re_hi, re_lo = split(w_re)
        im_hi, im_lo = split(w_im)
        for n, (re, im) in enumerate(((re_hi, im_hi), (re_lo, im_lo))):
            step_w[k, n, 0:U, 0:U] = re
            step_w[k, n, 0:U, U:] = -im
            step_w[k, n, U:, 0:U] = im
            step_w[k, n, U:, U:] = re
    row, col = iota((U, U), 0), iota((U, U), 1)
    at = iota((8, 2 * U), 0)
    at1 = iota((8, 1), 0)
    match = jnp.zeros((8, 2 * U), F32)
    cot = jnp.zeros((8, 2 * U), F32)
    for s in range(SUB):
        total = rx_ref[0, s].astype(F32)
        for p in range(1, NP // 2):
            total = total + rx_ref[p, s].astype(F32)
        tri = total[0:U]
        flip = tri.T
        g_re = jnp.where(row <= col, tri, flip)
        g_im = jnp.where(row > col, tri, jnp.where(row < col, -flip, 0.0))
        re_hi, re_lo = split(g_re)
        im_hi, im_lo = split(g_im)
        for n, (re, im) in enumerate(((re_hi, im_hi), (re_lo, im_lo))):
            gram_w[s, n, 0:U, 0:U] = re
            gram_w[s, n, 0:U, U:] = -im
            gram_w[s, n, U:, 0:U] = im
            gram_w[s, n, U:, U:] = re
        ext = total[U:ROWS]
        m_row = jnp.concatenate([ext[0:1] + ext[1:2], ext[2:3] + ext[3:4]], axis=1)
        c_row = jnp.concatenate([ext[4:5] + ext[5:6], ext[6:7] + ext[7:8]], axis=1)
        alive = (panel * SUB + s < count_ref[0]).astype(F32)
        match = jnp.where(at == s, jnp.broadcast_to(m_row, (8, 2 * U)), match)
        cot = jnp.where(at == s, jnp.broadcast_to(c_row * alive, (8, 2 * U)), cot)
    sigma = jnp.zeros((8, 1), F32)
    for s in range(SUB):
        sigma = jnp.where(at1 == s, noise_ref[panel * SUB + s], sigma)

    def parts(v):
        high, low = split(v)
        return jnp.concatenate([high, low], axis=0)

    def times_gram(v):
        both = parts(v)
        out = sigma * v
        for s in range(SUB):
            one = dot(both, gram_w[s, 0])
            two = dot(both, gram_w[s, 1])
            out = out + jnp.where(at == s, one[0:8] + one[8:16] + two[0:8], 0.0)
        return out

    def times_step(k, v, dims):
        both = parts(v)
        one = dot(both, step_w[k, 0], dims)
        two = dot(both, step_w[k, 1], dims)
        return one[0:8] + one[8:16] + two[0:8]

    def total_of(a, b):
        return jnp.sum(a * b, axis=1, keepdims=True)

    r = match
    energy = total_of(r, r) + EPS
    rs, ds, qs, es, al, cs, bs = [], [], [], [energy], [], [], []
    for k in range(3):
        d = r + times_step(k, r, NT)
        ratio = None
        if k > 0:
            ratio = es[k] / es[k - 1]
            d = d + ratio * ds[-1]
        q = times_gram(d)
        along = total_of(d, r)
        curve = total_of(d, q) + EPS
        alpha = along / curve
        rs.append(r)
        ds.append(d)
        qs.append(q)
        al.append(alpha)
        cs.append(curve)
        bs.append(ratio)
        if k < 2:
            r = r - alpha * q
            es.append(total_of(r, r) + EPS)

    qb, db = [None] * 3, [None] * 3
    rb = None
    d_next = None
    e_bar = [jnp.zeros((8, 1), F32) for _ in range(3)]
    for k in (2, 1, 0):
        a_bar = total_of(cot, ds[k])
        if rb is not None:
            a_bar = a_bar - total_of(rb, qs[k])
        along_bar = a_bar / cs[k]
        curve_bar = -along_bar * al[k]
        d_bar = al[k] * cot + along_bar * rs[k] + curve_bar * qs[k]
        if d_next is not None:
            d_bar = d_bar + d_next
        if rb is None:
            qb[k] = curve_bar * ds[k]
            d_bar = d_bar + curve_bar * qs[k]
            rb = along_bar * ds[k]
        else:
            qb[k] = curve_bar * ds[k] - al[k] * rb
            d_bar = d_bar + times_gram(qb[k])
            rb = rb + along_bar * ds[k]
        db[k] = d_bar
        rb = rb + d_bar + times_step(k, d_bar, NN)
        if k > 0:
            b_bar = total_of(d_bar, ds[k - 1]) / es[k - 1]
            e_bar[k] = e_bar[k] + b_bar
            e_bar[k - 1] = e_bar[k - 1] - b_bar * bs[k]
            d_next = bs[k] * d_bar
        rb = rb + 2.0 * e_bar[k] * rs[k]

    for s in range(SUB):
        block = rows_of([(v, s) for v in (qb[0], ds[0], qb[1], ds[1], qb[2], ds[2], rb)], 8)
        both = jnp.concatenate([block[:, 0:U], block[:, U:]], axis=0).astype(BF16)
        for p in range(NP):
            out_ref[p, 16 * s : 16 * s + 16, :] = both
    zeros = jnp.zeros((8, 2 * U), F32)
    for k in range(3):
        d_hi, d_lo = split(db[k])
        r_hi, r_lo = split(rs[k])
        left = jnp.concatenate([d_hi, d_lo, d_hi, zeros.astype(BF16)], axis=0)
        right = jnp.concatenate([r_hi, r_hi, r_lo, zeros.astype(BF16)], axis=0)
        outer = dot(left, right, TN)
        g_re = (outer[0:U, 0:U] + outer[U:, U:]).astype(BF16)
        g_im = (outer[U:, 0:U] - outer[0:U, U:]).astype(BF16)
        for p in range(NP):
            base = 64 + k * 32
            out_ref[p, base : base + 16, :] = g_re[16 * p : 16 * p + 16]
            out_ref[p, base + 16 : base + 32, :] = g_im[16 * p : 16 * p + 16]


def detect_call(noise, counts, rx, steps):
    smem = pl.BlockSpec(memory_space=pltpu.SMEM)
    vmem = pl.BlockSpec(memory_space=pltpu.VMEM)
    return pl.pallas_call(
        detect_kernel,
        out_shape=jax.ShapeDtypeStruct((NP, 160, U), BF16),
        in_specs=[smem, smem, vmem, vmem],
        out_specs=vmem,
        scratch_shapes=[
            pltpu.VMEM((SUB, 2, 2 * U, 2 * U), BF16),
            pltpu.VMEM((3, 2, 2 * U, 2 * U), BF16),
        ],
        compiler_params=pltpu.CompilerParams(vmem_limit_bytes=16 << 20),
        cost_estimate=pl.CostEstimate(flops=10**9, bytes_accessed=4 << 20, transcendentals=0),
        name="detect",
    )(noise, counts, rx, steps)


def chain_kernel(chan_ref, recv_ref, fac_ref, *rest):
    gchan_ref, grecv_ref = rest[-2:]
    at = iota((8, U), 0)
    even = iota((16, U), 0) % 2 == 0
    gy_re = jnp.zeros((8, A), F32)
    gy_im = jnp.zeros((8, A), F32)
    y_re, y_im = recv_ref[0].astype(F32), recv_ref[1].astype(F32)
    for j in range(8):
        s = j % SUB
        fac = fac_ref[j // SUB, 16 * s : 16 * s + 16, :]
        chan = jnp.concatenate([chan_ref[0, j], chan_ref[1, j]], axis=0)
        prod = dot(fac, chan, NT)
        v_re = prod[0:8, 0:A] - prod[8:16, A:]
        v_im = prod[0:8, A:] + prod[8:16, 0:A]
        gy_re = jnp.where(at == j, jnp.broadcast_to(v_re[6:7], (8, A)), gy_re)
        gy_im = jnp.where(at == j, jnp.broadcast_to(v_im[6:7], (8, A)), gy_im)
        v_re = jnp.where(at == 7, jnp.broadcast_to(y_re[j : j + 1], (8, A)), v_re)
        v_im = jnp.where(at == 7, jnp.broadcast_to(y_im[j : j + 1], (8, A)), v_im)
        re_hi, re_lo = split(v_re)
        im_hi, im_lo = split(v_im)
        left = jnp.concatenate([re_hi, im_hi, re_lo, im_lo], axis=0)
        wide = fac.astype(F32)
        down = jnp.concatenate([wide[1:16], wide[0:1]], axis=0)
        up = jnp.concatenate([wide[15:16], wide[0:15]], axis=0)
        mate = jnp.where(even, down, up)
        g_re, g_im = mate[0:8], mate[8:16]
        right = jnp.concatenate(
            [jnp.concatenate([g_re, -g_im], axis=1), jnp.concatenate([g_im, g_re], axis=1)], axis=0
        ).astype(BF16)
        right = jnp.concatenate([right, right], axis=0)
        out = dot(left, right, TN)
        gchan_ref[0, j] = out[:, 0:U].astype(BF16)
        gchan_ref[1, j] = out[:, U:].astype(BF16)
    grecv_ref[0] = gy_re.astype(BF16)
    grecv_ref[1] = gy_im.astype(BF16)


def chain_call(half, channel, received, factors, earlier=()):
    wide = pl.BlockSpec((2, 8, A, U), lambda i: (0, i + 2 * half, 0, 0))
    flat = pl.BlockSpec((2, 8, A), lambda i: (0, i + 2 * half, 0))
    return pl.pallas_call(
        chain_kernel,
        grid=(2,),
        out_shape=(
            jax.ShapeDtypeStruct((2, 32, A, U), BF16),
            jax.ShapeDtypeStruct((2, 32, A), BF16),
        ),
        in_specs=[wide, flat, pl.BlockSpec((2, 64, U), lambda i: (i + 2 * half, 0, 0))]
        + [pl.BlockSpec(memory_space=pl.ANY)] * len(earlier),
        out_specs=(wide, flat),
        input_output_aliases={3: 0, 4: 1} if earlier else {},
        compiler_params=pltpu.CompilerParams(vmem_limit_bytes=8 << 20),
        cost_estimate=pl.CostEstimate(flops=10**9, bytes_accessed=12 << 20, transcendentals=0),
        name="chain_b" if earlier else "chain_a",
    )(channel, received, factors, *earlier)


def widen_kernel(in_ref, out_ref):
    for p in range(NP):
        for k in range(6):
            rows = in_ref[p, 16 * k : 16 * k + 16, :].astype(F32)
            out_ref[k // 2, k % 2, 16 * p : 16 * p + 16, :] = rows


def widen_call(every):
    vmem = pl.BlockSpec(memory_space=pltpu.VMEM)
    return pl.pallas_call(
        widen_kernel,
        out_shape=jax.ShapeDtypeStruct((3, 2, U, U), F32),
        in_specs=[vmem],
        out_specs=vmem,
        compiler_params=pltpu.CompilerParams(vmem_limit_bytes=4 << 20),
        name="widen",
    )(every)


def exchange(value, axis, groups=None):
    return lax.all_to_all(
        value, axis, split_axis=0, concat_axis=0, tiled=True, axis_index_groups=groups
    )


def on_device(channel, received, noise, steps, cotangent, counts):
    z_groups = [[8 * z + y for z in range(8)] for y in range(8)]
    y_groups = [[8 * z + y for y in range(8)] for z in range(8)]
    cot = jnp.swapaxes(cotangent, 1, 2)
    away = gram_call(False, channel, received, cot)
    got = lax.ppermute(away, "panel", [(p, p ^ 1) for p in range(NP)])
    own = gram_call(True, channel, received, cot)
    pair = (own.astype(F32) + got.astype(F32)).astype(BF16)
    rx = exchange(pair, "panel", [[0, 2, 4, 6], [1, 3, 5, 7]])
    both = exchange(detect_call(noise, counts, rx, steps), "panel")
    part = jnp.sum(both[:, 64:].astype(F32), axis=0).astype(BF16)
    grads = ()
    for half, groups in enumerate((y_groups, z_groups)):
        grads = chain_call(half, channel, received, both, grads)
        every = exchange(jnp.broadcast_to(part, (8, 96, U)), "sc", groups)
        part = jnp.sum(every.astype(F32), axis=0).astype(BF16)
        part, grads = lax.optimization_barrier((part, grads))
    grad_channel, grad_received = grads
    every = exchange(jnp.broadcast_to(part, (8, 96, U)), "panel")
    return (grad_channel, grad_received, widen_call(every))


def solution(mesh):
    return jax.shard_map(
        on_device,
        mesh=mesh,
        in_specs=(
            P(None, "sc", "panel", None),
            P(None, "sc", "panel"),
            P("sc"),
            P(),
            P(None, "sc", "panel"),
            P("sc"),
        ),
        out_specs=(P(None, "sc", "panel", None), P(None, "sc", "panel"), P()),
        check_vma=False,
    )
```
